512 devices in a mesh: dp: 32 (over z, x), tensor: 16 (over y, core).
Axes of the slice: x: 4, y: 8, z: 8, core: 2. Of those that a mesh axis runs over, the one named last changes fastest.
Arguments:
- teacher_hidden: bfloat16 [512, 5120], P('dp', 'tensor'), may hold values from -200 to 200
- student_hidden: bfloat16 [512, 4096], P('dp', 'tensor'), may hold values from -8 to 8
- teacher_head: bfloat16 [5120, 131072], P(None, ('dp', 'tensor')), may hold values from -6 to 6
- student_head: bfloat16 [4096, 131072], P(None, ('dp', 'tensor')), may hold values from -6 to 6
- teacher_gain: float32 [5120], replicated, may hold values from 0.5 to 1.5
- lengths: int32 [64], replicated, may hold values from 1 to 8, as said below
- student_row: int32 [512], replicated, may hold values from 0 to 511, as said below
- targets: int32 [512], replicated, may hold values from 0 to 131071
Outputs:
- grad_logits: bfloat16 [512, 131072], P(None, ('dp', 'tensor'))
- divergence: float32 [512], P('dp')
- log_ratio: float32 [512], P('dp')
The draws below stay inside these ranges and needn't reach their ends.
Inputs may be any that keep to these rules, and one draw needn't show every extreme that they name: The lengths of the 2 responses of one index of dp sum to at most 8, and to exactly 8 on some index. `student_row`: a permutation: every row of student_hidden is named once.
All inputs are finite; a program needn't handle non-finite values.
Results may differ from the reference program's by a relative error of at most 0.01095.
Values may be sent and summed in bfloat16 or wider, within the bound.
No kernel may reach another device: no remote copies, remote signals or barrier semaphores. Data moves between devices by JAX's collectives and lax.ppermute only.
A program may use at most 64 MiB of HBM per device.

```python
import math
import jax
import jax.numpy as jnp
import numpy as np
from jax import lax

DT = 5120
DS = 4096
SLOT = 8
SEQ_DEV = 2
LIVE_DEV = 8
SEQS = 64
TOKENS = 512
VOCAB = 131072


paired_count = 6


planted_score = 200.0


def pairing(key):
    base = jax.random.fold_in(key, 7)
    keys = jax.random.split(base, 6)
    token_rows = jax.random.randint(keys[0], (paired_count,), 0, TOKENS)
    columns = jax.random.randint(keys[1], (paired_count,), 0, VOCAB - 1)
    strength = jax.random.uniform(keys[2], (paired_count,), jnp.float32, 0.6, 1.15).at[0].set(1.15)
    teacher_gap = jax.random.uniform(keys[3], (paired_count,), jnp.float32, 1.0, 3.0)
    student_gap = jax.random.uniform(keys[4], (paired_count,), jnp.float32, 1.0, 3.0)
    order = jax.random.permutation(keys[5], TOKENS).astype(jnp.int32)
    return (token_rows, columns, strength, teacher_gap, student_gap, order)


def teacher_values(key):
    inner = jax.random.fold_in(key, 21)
    return jnp.clip(jax.random.normal(inner, (TOKENS, DT), jnp.float32), -6.0, 6.0)


def student_values(key):
    inner = jax.random.fold_in(key, 31)
    return jnp.clip(jax.random.normal(inner, (TOKENS, DS), jnp.float32), -6.0, 6.0)


def base_head(key, width, depth):
    return jnp.clip(jax.random.normal(key, (depth, VOCAB), jnp.float32), -6.0, 6.0) * width


def draw_teacher_hidden(key, part):
    return teacher_values(key).astype(jnp.bfloat16)


def draw_student_hidden(key, part):
    return student_values(key).astype(jnp.bfloat16)


def draw_teacher_head(key, part):
    width = 3.0 / math.sqrt(DT)
    head = base_head(jax.random.fold_in(key, 22), width, DT)
    token_rows, columns, strength, teacher_gap, student_gap, order = pairing(key)
    chosen = teacher_values(key)[token_rows]
    unit_rows = chosen * lax.rsqrt(jnp.mean(chosen * chosen, axis=1, keepdims=True))
    nominal = planted_score * strength
    column = unit_rows * (nominal / DT)[:, None]
    second = column * (1.0 - teacher_gap / nominal)[:, None]
    head = head.at[:, columns].set(column.T)
    head = head.at[:, columns + 1].set(second.T)
    return head.astype(jnp.bfloat16)


def draw_student_head(key, part):
    width = 3.0 / math.sqrt(DS)
    head = base_head(jax.random.fold_in(key, 32), width, DS)
    token_rows, columns, strength, teacher_gap, student_gap, order = pairing(key)
    chosen = student_values(key)[order[token_rows]]
    nominal = planted_score * strength
    column = chosen / jnp.mean(chosen * chosen, axis=1, keepdims=True) * (nominal / DS)[:, None]
    second = column * (1.0 - student_gap / nominal)[:, None]
    head = head.at[:, columns].set(column.T)
    head = head.at[:, columns + 1].set(second.T)
    return head.astype(jnp.bfloat16)


def draw_student_row(key, part):
    return pairing(key)[5]


def draw_lengths(key, part):
    inner = jax.random.fold_in(key, 41)
    keys = jax.random.split(inner, 2)
    groups = SEQS // SEQ_DEV
    raw_lengths = jax.random.randint(keys[0], (groups, SEQ_DEV), 1, SLOT + 1)
    busiest = jax.random.randint(keys[1], (), 0, groups)
    raw_lengths = jnp.where(jnp.arange(groups)[:, None] == busiest, SLOT, raw_lengths)
    used = jnp.zeros((groups,), jnp.int32)
    columns = []
    for number in range(SEQ_DEV):
        room = LIVE_DEV - (SEQ_DEV - 1 - number) - used
        length_now = jnp.minimum(raw_lengths[:, number], room)
        used = used + length_now
        columns.append(length_now)
    return jnp.stack(columns, axis=1).reshape(SEQS).astype(jnp.int32)


def set_ends(drawn, key, smallest, largest):
    extent = drawn.shape
    index_at = [jax.random.randint(jax.random.fold_in(key, axis), (), 0, extent[axis]) for axis in range(len(extent))]
    drawn = drawn.at[tuple(index_at)].set(smallest)
    longest = extent.index(max(extent))
    index_at[longest] = (index_at[longest] + 1) % extent[longest]
    return drawn.at[tuple(index_at)].set(largest)


def skewed_wide(rng, dims, amount, lean):
    loads = [min(1 << octave, amount + 1 - (1 << octave)) * (1 << 20) // math.isqrt((1 << octave) ** lean) + 1 for octave in range((amount + 1).bit_length()) if 1 << octave <= amount]
    deviation = 1 + sum(loads) // (1 << 30)
    grid = np.cumsum(np.array([max(1, weight // deviation) for weight in loads]))
    lot = jax.random.randint(jax.random.fold_in(rng, 1), dims, 0, int(grid[len(loads) - 1]))
    start = jnp.left_shift(1, jnp.searchsorted(jnp.asarray(grid, jnp.int32), lot, side="right").astype(jnp.int32))
    standing = start - 1 + jax.random.randint(jax.random.fold_in(rng, 4), dims, 0, 1 << 30) % jnp.minimum(start, amount + 1 - start)
    return jax.random.permutation(jax.random.fold_in(rng, 2), amount)[standing].astype(jnp.int32)


def setup_inputs(seed: int = 0) -> dict:
    arg_keys = jax.random.split(jax.random.key(seed), 9)
    teacher_hidden = draw_teacher_hidden(jax.random.fold_in(arg_keys[8], 71), 0)
    student_hidden = draw_student_hidden(jax.random.fold_in(arg_keys[8], 71), 0)
    teacher_head = draw_teacher_head(jax.random.fold_in(arg_keys[8], 71), 0)
    student_head = draw_student_head(jax.random.fold_in(arg_keys[8], 71), 0)
    teacher_gain = jnp.clip(1.0 + 0.1 * jax.random.normal(arg_keys[4], (DT,), jnp.float32), 0.5, 1.5)
    lengths = draw_lengths(jax.random.fold_in(arg_keys[8], 71), 0)
    student_row = draw_student_row(jax.random.fold_in(arg_keys[8], 71), 0)
    targets = set_ends(skewed_wide(arg_keys[7], (TOKENS,), VOCAB, 2), jax.random.fold_in(arg_keys[7], 3), 0, VOCAB - 1).astype(jnp.int32)
    return {"teacher_hidden": teacher_hidden, "student_hidden": student_hidden, "teacher_head": teacher_head, "student_head": student_head, "teacher_gain": teacher_gain, "lengths": lengths, "student_row": student_row, "targets": targets}


def reference(teacher_hidden, student_hidden, teacher_head, student_head, teacher_gain, lengths, student_row, targets):
    token_count = teacher_hidden.shape[0]
    token_ids = jnp.arange(token_count, dtype=jnp.int32)
    live_mask = (token_ids % SLOT < lengths[token_ids // SLOT]).astype(jnp.float32)
    hidden_rows = teacher_hidden.astype(jnp.float32)
    row_scale = lax.rsqrt(lax.optimization_barrier(jnp.mean(hidden_rows * hidden_rows, axis=1, keepdims=True)) + 1e-06)
    normed = (hidden_rows * row_scale * teacher_gain[None, :]).astype(jnp.bfloat16)
    teacher_logits = jnp.dot(normed, teacher_head, preferred_element_type=jnp.float32)
    student_logits = jnp.dot(student_hidden[student_row], student_head, preferred_element_type=jnp.float32)
    teacher_logp = teacher_logits - jax.nn.logsumexp(teacher_logits, axis=1)[:, None]
    student_logp = student_logits - jax.nn.logsumexp(student_logits, axis=1)[:, None]
    student_prob = jnp.exp(student_logp)
    kl_raw = lax.optimization_barrier(jnp.sum(student_prob * (student_logp - teacher_logp), axis=1))
    picked_student = jnp.take_along_axis(student_logp, targets[:, None], axis=1)[:, 0]
    picked_teacher = jnp.take_along_axis(teacher_logp, targets[:, None], axis=1)[:, 0]
    log_ratio = live_mask * (picked_student - picked_teacher)
    gradient = live_mask[:, None] * student_prob * (student_logp - teacher_logp - kl_raw[:, None])
    return (gradient.astype(jnp.bfloat16), live_mask * kl_raw, log_ratio)
```

```python
import jax
import jax.numpy as jnp
from jax import lax
from jax.sharding import Mesh
from jax.sharding import PartitionSpec as P

SLOT = 8
LIVE_DEV = 8
DP = ("dp_0", "dp_1")
TENSOR = ("tensor_0", "tensor_1")
DP_TENSOR = ("dp_0", "dp_1", "tensor_0", "tensor_1")


def spread(array, axes):
    count = lax.axis_size(axes)
    return lax.all_to_all(jnp.broadcast_to(array, (count, *array.shape)), axes, 0, 0)


def shifted(array, axis, by):
    count = lax.axis_size(axis)
    return lax.ppermute(array, axis, [(i, (i + by) % count) for i in range(count)])


def ring_pieces(piece, axis):
    count = lax.axis_size(axis)
    half = piece.shape[0] // 2
    found = [(0, 0, piece)]
    ahead = behind = piece
    for k in range(1, count // 2):
        ahead, behind = shifted(ahead, axis, 1), shifted(behind, axis, -1)
        found += [(-k, 0, ahead), (k, 0, behind)]
    last = [shifted(ahead[:half], axis, 1), shifted(behind[half:], axis, -1)]
    found.append((count // 2, 0, jnp.concatenate(last, axis=0)))
    return found


def merge(parts):
    teacher, student, mean, picked = (parts[:, k] for k in range(4))
    top_t, top_s = jnp.max(teacher, axis=0), jnp.max(student, axis=0)
    sum_t = jnp.sum(jnp.exp(teacher - top_t), axis=0)
    weight = jnp.exp(student - top_s)
    sum_s = jnp.sum(weight, axis=0)
    mean = jnp.sum(weight * mean, axis=0) / sum_s
    return jnp.stack([top_t + jnp.log(sum_t), top_s + jnp.log(sum_s), mean, jnp.sum(picked, axis=0)])


def on_device(
    teacher_hidden,
    student_hidden,
    teacher_head,
    student_head,
    teacher_gain,
    lengths,
    student_row,
    targets,
):
    dp_count = lax.axis_size(DP)
    tensor_count = lax.axis_size(TENSOR)
    y_count, core_count = (lax.axis_size(a) for a in TENSOR)
    local_tokens, t_width = teacher_hidden.shape
    s_width = student_hidden.shape[1]
    token_count = local_tokens * dp_count
    vocab_local = teacher_head.shape[1]
    dp_index = lax.axis_index(DP)
    y_index, core = lax.axis_index("tensor_0"), lax.axis_index("tensor_1")
    vocab_start = (dp_index * tensor_count + lax.axis_index(TENSOR)) * vocab_local

    t_blocks = teacher_head.reshape(y_count, core_count, t_width, vocab_local)
    s_blocks = student_head.reshape(y_count, core_count, s_width, vocab_local)
    pick = lambda blocks, c: lax.dynamic_index_in_dim(blocks, c, 1, keepdims=False)
    t_heads = jnp.concatenate(
        [pick(t_blocks, core), shifted(pick(t_blocks, 1 - core), "tensor_1", 1)], axis=2
    )
    s_heads = jnp.concatenate(
        [pick(s_blocks, core), shifted(pick(s_blocks, 1 - core), "tensor_1", 1)], axis=2
    )
    gains = pick(teacher_gain.reshape(y_count, core_count, t_width), core)

    first, second = lengths.reshape(dp_count, 2)[:, :1], lengths.reshape(dp_count, 2)[:, 1:]
    slot = jnp.arange(LIVE_DEV, dtype=jnp.int32)[None, :]
    place = jnp.where(slot < first, slot, SLOT + slot - first)
    live = slot < first + second
    group = jnp.arange(dp_count, dtype=jnp.int32)[:, None] * local_tokens
    row_token = jnp.where(live, group + place, -1).reshape(-1)
    row_live = live.reshape(-1).astype(jnp.float32)
    rows = row_token.shape[0]

    own = lax.dynamic_slice_in_dim(row_token, dp_index * LIVE_DEV, LIVE_DEV) - dp_index * local_tokens
    own_picks = own[:, None] == jnp.arange(local_tokens, dtype=jnp.int32)[None, :]
    teacher_local = jnp.dot(
        own_picks.astype(jnp.bfloat16), teacher_hidden, preferred_element_type=jnp.float32
    ).astype(jnp.bfloat16)
    half = local_tokens // 2
    packed = jnp.concatenate([student_hidden[:half], student_hidden[half:], teacher_local], axis=1)
    everyone = spread(packed, DP)

    token_of = row_token[:, None] == jnp.arange(token_count, dtype=jnp.int32)[None, :]
    row_source = jnp.sum(jnp.where(token_of, student_row[None, :], 0), axis=1)
    row_target = jnp.sum(jnp.where(token_of, targets[None, :], 0), axis=1)
    j = jnp.arange(token_count // 2, dtype=jnp.int32)
    low = (j // half) * local_tokens + j % half
    source_of = row_source[:, None] == jnp.concatenate([low, low + half])[None, :]
    student_rows = jnp.concatenate(
        [everyone[:, :, :s_width], everyone[:, :, s_width : 2 * s_width]], axis=0
    ).reshape(token_count, s_width)
    chosen = jnp.dot(
        source_of.astype(jnp.bfloat16), student_rows, preferred_element_type=jnp.float32
    ).astype(jnp.bfloat16)
    piece = jnp.concatenate([chosen, everyone[:, :, 2 * s_width :].reshape(rows, t_width)], axis=1)

    t_part = s_part = squares = 0.0
    for offset, _, block in ring_pieces(piece, "tensor_0"):
        at = (y_index + offset) % y_count
        take = lambda heads: lax.dynamic_index_in_dim(heads, at, 0, keepdims=False)
        s_part += jnp.dot(block[:, :s_width], take(s_heads), preferred_element_type=jnp.float32)
        values = block[:, s_width:].astype(jnp.float32)
        squares += jnp.sum(values * values, axis=1, keepdims=True)
        scaled = (values * take(gains)[None, :]).astype(jnp.bfloat16)
        t_part += jnp.dot(scaled, take(t_heads), preferred_element_type=jnp.float32)
    mine = jnp.concatenate([t_part[:, :vocab_local], s_part[:, :vocab_local]], axis=1)
    sent = jnp.concatenate(
        [t_part[:, vocab_local:], s_part[:, vocab_local:], jnp.broadcast_to(squares, (rows, 128))],
        axis=1,
    )
    got = shifted(sent, "tensor_1", 1)
    mean_square = (squares + got[:, 2 * vocab_local :][:, :1]) / (t_width * tensor_count)
    row_scale = lax.rsqrt(mean_square + 1e-06)
    both = mine + got[:, : 2 * vocab_local]
    teacher_logits = both[:, :vocab_local] * row_scale
    student_logits = both[:, vocab_local:]

    gap = student_logits - teacher_logits
    hits = (row_target - vocab_start)[:, None] == jnp.arange(vocab_local, dtype=jnp.int32)[None, :]
    picked = jnp.sum(jnp.where(hits, gap, 0.0), axis=1)
    teacher_max = jnp.max(teacher_logits, axis=1)
    student_max = jnp.max(student_logits, axis=1)
    teacher_sum = jnp.sum(jnp.exp(teacher_logits - teacher_max[:, None]), axis=1)
    student_exp = jnp.exp(student_logits - student_max[:, None])
    student_sum = jnp.sum(student_exp, axis=1)
    mean = jnp.sum(student_exp * gap, axis=1) / student_sum
    local = jnp.stack(
        [teacher_max + jnp.log(teacher_sum), student_max + jnp.log(student_sum), mean, picked]
    )
    merged = merge(spread(merge(spread(local, DP)), TENSOR))
    teacher_lse, student_lse, mean, picked = (merged[k] for k in range(4))

    student_prob = jnp.exp(student_logits - student_lse[:, None])
    gradient = (row_live[:, None] * student_prob * (gap - mean[:, None])).astype(jnp.bfloat16)
    lse_gap = teacher_lse - student_lse
    token_ids = jnp.arange(token_count, dtype=jnp.int32)
    unpack = (token_ids[:, None] == row_token[None, :]).astype(jnp.bfloat16)
    grad_logits = jnp.dot(unpack, gradient, preferred_element_type=jnp.float32).astype(jnp.bfloat16)
    own_ids = dp_index * local_tokens + jnp.arange(local_tokens, dtype=jnp.int32)
    own_of = own_ids[:, None] == row_token[None, :]
    divergence = jnp.sum(jnp.where(own_of, (mean + lse_gap)[None, :], 0.0), axis=1)
    log_ratio = jnp.sum(jnp.where(own_of, (picked + lse_gap)[None, :], 0.0), axis=1)
    return (grad_logits, divergence, log_ratio)


def solution(mesh):
    finer = Mesh(mesh.devices.reshape(8, 4, 8, 2), ("dp_0", "dp_1", "tensor_0", "tensor_1"))
    in_specs = (
        P(DP, TENSOR),
        P(DP, TENSOR),
        P(None, DP_TENSOR),
        P(None, DP_TENSOR),
        P(),
        P(),
        P(),
        P(),
    )
    out_specs = (P(None, DP_TENSOR), P(DP), P(DP))
    return jax.shard_map(
        on_device, mesh=finer, in_specs=in_specs, out_specs=out_specs, check_vma=False
    )
```

```python
import functools

import jax
import jax.numpy as jnp
from jax import lax
from jax.experimental import pallas as pl
from jax.experimental.pallas import tpu as pltpu
from jax.sharding import Mesh
from jax.sharding import PartitionSpec as P


SLOT = 8
LIVE_DEV = 8
DP = ("dp_0", "dp_1")
TENSOR = ("tensor_0", "tensor_1")
DP_TENSOR = ("dp_0", "dp_1", "tensor_0", "tensor_1")


def spread(array, axes):
    count = lax.axis_size(axes)
    return lax.all_to_all(jnp.broadcast_to(array, (count, *array.shape)), axes, 0, 0)


def shifted(array, axis, by):
    count = lax.axis_size(axis)
    return lax.ppermute(array, axis, [(i, (i + by) % count) for i in range(count)])


def ring_pieces(piece, axis):
    count = lax.axis_size(axis)
    found = [(0, piece)]
    ahead = behind = piece
    for k in range(1, count // 2):
        ahead, behind = shifted(ahead, axis, 1), shifted(behind, axis, -1)
        found += [(-k, ahead), (k, behind)]
    return found + [(-(count // 2), shifted(ahead, axis, 1))]


VMEM = pl.BlockSpec(memory_space=pltpu.VMEM)
SMEM = pl.BlockSpec(memory_space=pltpu.SMEM)
ANY = pl.BlockSpec(memory_space=pl.ANY)
TERMS = 3


def pack_kernel(lengths, teacher, student, packed):
    group = lax.axis_index("dp_0") * lax.axis_size("dp_1") + lax.axis_index("dp_1")
    first, second = lengths[2 * group], lengths[2 * group + 1]
    half, s_width = student.shape[0] // 2, student.shape[1]
    grid = (LIVE_DEV, teacher.shape[0])
    slot, row = (lax.broadcasted_iota(jnp.int32, grid, d) for d in range(2))
    place = jnp.where(slot < first, slot, SLOT + slot - first)
    pick = jnp.where((place == row) & (slot < first + second), 1.0, 0.0)
    chosen = jnp.dot(
        pick.astype(jnp.bfloat16), teacher[...], preferred_element_type=jnp.float32
    ).astype(jnp.bfloat16)
    low, high = student[:half, :], student[half:, :]
    for i in range(packed.shape[0]):
        packed[i, :, :s_width] = low
        packed[i, :, s_width : 2 * s_width] = high
        packed[i, :, 2 * s_width :] = chosen


def choose_kernel(half, s_width, source, gains, everyone, piece):
    count = everyone.shape[0]
    t_width = everyone.shape[1] - 2 * s_width
    wide = lax.axis_index("tensor_0") * lax.axis_size("tensor_1") + lax.axis_index("tensor_1")
    j = lax.broadcasted_iota(jnp.int32, (count, count), 1)
    low = (j // half) * (2 * half) + j % half
    want = jnp.broadcast_to(source[:, :1], (count, count))
    one = lambda hit: jnp.where(hit, 1.0, 0.0).astype(jnp.bfloat16)
    dot = functools.partial(jnp.dot, preferred_element_type=jnp.float32)
    chosen = dot(one(want == low), everyone[:, :s_width])
    chosen += dot(one(want == low + half), everyone[:, s_width : 2 * s_width])
    piece[:, :s_width] = chosen.astype(jnp.bfloat16)
    values = everyone[:, 2 * s_width :].astype(jnp.float32)
    piece[:, s_width : s_width + t_width] = (values * gains[pl.ds(wide, 1), :]).astype(jnp.bfloat16)
    rest = jnp.sum(values * values, axis=1, keepdims=True)
    at = s_width + t_width
    for k in range(TERMS):
        term = rest.astype(jnp.bfloat16)
        piece[:, at + k : at + k + 1] = term
        rest = rest - term.astype(jnp.float32)


def block_kernel(offsets, had, t_width, s_width, *refs):
    n = len(offsets)
    blocks, refs = refs[:n], refs[n:]
    t_head, s_head, t_twin, s_twin = refs[:4]
    refs = refs[4:]
    if had:
        before, refs = refs[:2], refs[2:]
    mine, sent, t_own_buf, s_own_buf, t_twin_buf, s_twin_buf, sems = refs
    y, core = lax.axis_index("tensor_0"), lax.axis_index("tensor_1")
    ys, cores = lax.axis_size("tensor_0"), lax.axis_size("tensor_1")
    vocab = t_head.shape[1]
    copies = []
    for i, offset in enumerate(offsets):
        at = lax.rem(y + (offset % ys), ys)
        wide = at * cores + core
        froms = (
            t_head.at[pl.ds(pl.multiple_of(wide * t_width, 64), t_width), :],
            s_head.at[pl.ds(pl.multiple_of(wide * s_width, 64), s_width), :],
            t_twin.at[at],
            s_twin.at[at],
        )
        tos = (t_own_buf.at[i], s_own_buf.at[i], t_twin_buf.at[i], s_twin_buf.at[i])
        for k in range(4):
            copy = pltpu.make_async_copy(froms[k], tos[k], sems.at[i, k])
            copy.start()
            copies.append(copy)
    t_mine = s_mine = t_sent = s_sent = squares = None
    dot = functools.partial(jnp.dot, preferred_element_type=jnp.float32)
    if had:
        t_mine, s_mine = before[0][:, :vocab], before[0][:, vocab:]
        t_sent, s_sent = before[1][:, :vocab], before[1][:, vocab : 2 * vocab]
        squares = before[1][:, 2 * vocab : 2 * vocab + 1]
    plus = lambda total, term: term if total is None else total + term
    for i in range(n):
        for k in range(4):
            copies[4 * i + k].wait()
        at = s_width + t_width
        for k in range(TERMS):
            squares = plus(squares, blocks[i][:, at + k : at + k + 1].astype(jnp.float32))
        student, scaled = blocks[i][:, :s_width], blocks[i][:, s_width:at]
        t_mine = plus(t_mine, dot(scaled, t_own_buf[i]))
        t_sent = plus(t_sent, dot(scaled, t_twin_buf[i]))
        s_mine = plus(s_mine, dot(student, s_own_buf[i]))
        s_sent = plus(s_sent, dot(student, s_twin_buf[i]))
    mine[:, :vocab], mine[:, vocab:] = t_mine, s_mine
    sent[:, :vocab], sent[:, vocab : 2 * vocab] = t_sent, s_sent
    sent[:, 2 * vocab :] = jnp.broadcast_to(squares, (squares.shape[0], 128))


def block_products(found, heads, before):
    offsets, blocks = [f[0] for f in found], [f[1] for f in found]
    n, rows, vocab = len(found), blocks[0].shape[0], heads[0].shape[1]
    t_width, s_width = heads[2].shape[1], heads[3].shape[1]
    had = before is not None
    bf16 = jnp.bfloat16
    return pl.pallas_call(
        functools.partial(block_kernel, offsets, had, t_width, s_width),
        out_shape=(
            jax.ShapeDtypeStruct((rows, 2 * vocab), jnp.float32),
            jax.ShapeDtypeStruct((rows, 2 * vocab + 128), jnp.float32),
        ),
        in_specs=[VMEM] * n + [ANY] * 4 + [VMEM] * (2 if had else 0),
        out_specs=(VMEM, VMEM),
        scratch_shapes=[
            pltpu.VMEM((n, t_width, vocab), bf16),
            pltpu.VMEM((n, s_width, vocab), bf16),
            pltpu.VMEM((n, t_width, vocab), bf16),
            pltpu.VMEM((n, s_width, vocab), bf16),
            pltpu.SemaphoreType.DMA((n, 4)),
        ],
        compiler_params=pltpu.CompilerParams(vmem_limit_bytes=24 << 20),
        cost_estimate=pl.CostEstimate(
            flops=4 * n * rows * vocab * (t_width + s_width),
            bytes_accessed=4 * n * vocab * (t_width + s_width),
            transcendentals=0,
        ),
    )(*blocks, *heads, *(before if had else ()))


def merge(parts):
    teacher, student, mean, picked = (parts[:, k] for k in range(4))
    top_t, top_s = jnp.max(teacher, axis=0), jnp.max(student, axis=0)
    sum_t = jnp.sum(jnp.exp(teacher - top_t), axis=0)
    weight = jnp.exp(student - top_s)
    sum_s = jnp.sum(weight, axis=0)
    mean = jnp.sum(weight * mean, axis=0) / sum_s
    return jnp.stack([top_t + jnp.log(sum_t), top_s + jnp.log(sum_s), mean, jnp.sum(picked, axis=0)])


def on_device(
    teacher_hidden,
    student_hidden,
    teacher_head,
    student_head,
    teacher_gain,
    lengths,
    student_row,
    targets,
):
    dp_count = lax.axis_size(DP)
    tensor_count = lax.axis_size(TENSOR)
    y_count, core_count = (lax.axis_size(a) for a in TENSOR)
    local_tokens, t_width = teacher_hidden.shape
    s_width = student_hidden.shape[1]
    token_count = local_tokens * dp_count
    vocab_local = teacher_head.shape[1]
    dp_index = lax.axis_index(DP)
    core = lax.axis_index("tensor_1")
    vocab_start = (dp_index * tensor_count + lax.axis_index(TENSOR)) * vocab_local

    first, second = lengths.reshape(dp_count, 2)[:, :1], lengths.reshape(dp_count, 2)[:, 1:]
    slot = jnp.arange(LIVE_DEV, dtype=jnp.int32)[None, :]
    place = jnp.where(slot < first, slot, SLOT + slot - first)
    live = slot < first + second
    group = jnp.arange(dp_count, dtype=jnp.int32)[:, None] * local_tokens
    row_token = jnp.where(live, group + place, -1).reshape(-1)
    row_live = live.reshape(-1).astype(jnp.float32)
    rows = row_token.shape[0]

    half = local_tokens // 2
    packed = pl.pallas_call(
        pack_kernel,
        out_shape=jax.ShapeDtypeStruct((dp_count, half, 2 * s_width + t_width), jnp.bfloat16),
        in_specs=[SMEM, VMEM, VMEM],
        out_specs=VMEM,
        compiler_params=pltpu.CompilerParams(vmem_limit_bytes=8 << 20),
    )(lengths, teacher_hidden, student_hidden)
    t_blocks = teacher_head.reshape(y_count, core_count, t_width, vocab_local)
    s_blocks = student_head.reshape(y_count, core_count, s_width, vocab_local)
    other = lambda blocks: lax.dynamic_index_in_dim(blocks, 1 - core, 1, keepdims=False)
    twins = [shifted(other(blocks), "tensor_1", 1) for blocks in (t_blocks, s_blocks)]
    heads = (teacher_head, student_head, *twins)
    gains = teacher_gain.reshape(tensor_count, t_width)
    everyone = lax.all_to_all(packed, DP, 0, 0)

    token_of = row_token[:, None] == jnp.arange(token_count, dtype=jnp.int32)[None, :]
    row_source = jnp.sum(jnp.where(token_of, student_row[None, :], 0), axis=1)
    row_target = jnp.sum(jnp.where(token_of, targets[None, :], 0), axis=1)
    piece = pl.pallas_call(
        functools.partial(choose_kernel, half, s_width),
        out_shape=jax.ShapeDtypeStruct((rows, s_width + t_width + TERMS), jnp.bfloat16),
        in_specs=[VMEM] * 3,
        out_specs=VMEM,
        compiler_params=pltpu.CompilerParams(vmem_limit_bytes=8 << 20),
    )(jnp.broadcast_to(row_source[:, None], (rows, 128)), gains, everyone.reshape(rows, -1))

    found = ring_pieces(piece, "tensor_0")
    early = 1 + 2 * 2
    mine, sent = block_products(found[:early], heads, None)
    mine, sent = block_products(found[early:], heads, (mine, sent))
    squares = sent[:, 2 * vocab_local :][:, :1]
    got = shifted(sent, "tensor_1", 1)
    mean_square = (squares + got[:, 2 * vocab_local :][:, :1]) / (t_width * tensor_count)
    row_scale = lax.rsqrt(mean_square + 1e-06)
    both = mine + got[:, : 2 * vocab_local]
    teacher_logits = both[:, :vocab_local] * row_scale
    student_logits = both[:, vocab_local:]

    gap = student_logits - teacher_logits
    hits = (row_target - vocab_start)[:, None] == jnp.arange(vocab_local, dtype=jnp.int32)[None, :]
    picked = jnp.sum(jnp.where(hits, gap, 0.0), axis=1)
    teacher_max = jnp.max(teacher_logits, axis=1)
    student_max = jnp.max(student_logits, axis=1)
    teacher_sum = jnp.sum(jnp.exp(teacher_logits - teacher_max[:, None]), axis=1)
    student_exp = jnp.exp(student_logits - student_max[:, None])
    student_sum = jnp.sum(student_exp, axis=1)
    mean = jnp.sum(student_exp * gap, axis=1) / student_sum
    local = jnp.stack(
        [teacher_max + jnp.log(teacher_sum), student_max + jnp.log(student_sum), mean, picked]
    )
    merged = merge(spread(merge(spread(local, DP)), TENSOR))
    teacher_lse, student_lse, mean, picked = (merged[k] for k in range(4))

    student_prob = jnp.exp(student_logits - student_lse[:, None])
    gradient = (row_live[:, None] * student_prob * (gap - mean[:, None])).astype(jnp.bfloat16)
    lse_gap = teacher_lse - student_lse
    token_ids = jnp.arange(token_count, dtype=jnp.int32)
    unpack = (token_ids[:, None] == row_token[None, :]).astype(jnp.bfloat16)
    grad_logits = jnp.dot(unpack, gradient, preferred_element_type=jnp.float32).astype(jnp.bfloat16)
    own_ids = dp_index * local_tokens + jnp.arange(local_tokens, dtype=jnp.int32)
    own_of = own_ids[:, None] == row_token[None, :]
    divergence = jnp.sum(jnp.where(own_of, (mean + lse_gap)[None, :], 0.0), axis=1)
    log_ratio = jnp.sum(jnp.where(own_of, (picked + lse_gap)[None, :], 0.0), axis=1)
    return (grad_logits, divergence, log_ratio)


def solution(mesh):
    finer = Mesh(mesh.devices.reshape(8, 4, 8, 2), ("dp_0", "dp_1", "tensor_0", "tensor_1"))
    in_specs = (
        P(DP, TENSOR),
        P(DP, TENSOR),
        P(None, DP_TENSOR),
        P(None, DP_TENSOR),
        P(),
        P(),
        P(),
        P(),
    )
    out_specs = (P(None, DP_TENSOR), P(DP), P(DP))
    return jax.shard_map(
        on_device, mesh=finer, in_specs=in_specs, out_specs=out_specs, check_vma=False
    )
```

```python
import functools

import jax
import jax.numpy as jnp
from jax import lax
from jax.experimental import pallas as pl
from jax.experimental.pallas import tpu as pltpu
from jax.sharding import Mesh
from jax.sharding import PartitionSpec as P


SLOT = 8
LIVE_DEV = 8
DP = ("dp_0", "dp_1")
TENSOR = ("tensor_0", "tensor_1")
DP_TENSOR = ("dp_0", "dp_1", "tensor_0", "tensor_1")


def spread(array, axes):
    count = lax.axis_size(axes)
    return lax.all_to_all(jnp.broadcast_to(array, (count, *array.shape)), axes, 0, 0)


def shifted(array, axis, by):
    count = lax.axis_size(axis)
    return lax.ppermute(array, axis, [(i, (i + by) % count) for i in range(count)])


def ring_pieces(piece, axis):
    count = lax.axis_size(axis)
    found = [(0, piece)]
    ahead = behind = piece
    for k in range(1, count // 2):
        ahead = shifted(ahead, axis, 1)
        behind = shifted(behind, axis, -1)
        found += [(-k, ahead), (k, behind)]
    return found + [(-(count // 2), shifted(ahead, axis, 1))]


VMEM = pl.BlockSpec(memory_space=pltpu.VMEM)
SMEM = pl.BlockSpec(memory_space=pltpu.SMEM)
ANY = pl.BlockSpec(memory_space=pl.ANY)
TERMS = 3


def pack_kernel(lengths, teacher, student, packed):
    group = lax.axis_index("dp_0") * lax.axis_size("dp_1") + lax.axis_index("dp_1")
    first, second = lengths[2 * group], lengths[2 * group + 1]
    half, s_width = student.shape[0] // 2, student.shape[1]
    grid = (LIVE_DEV, teacher.shape[0])
    slot, row = (lax.broadcasted_iota(jnp.int32, grid, d) for d in range(2))
    place = jnp.where(slot < first, slot, SLOT + slot - first)
    pick = jnp.where((place == row) & (slot < first + second), 1.0, 0.0)
    chosen = jnp.dot(
        pick.astype(jnp.bfloat16), teacher[...], preferred_element_type=jnp.float32
    ).astype(jnp.bfloat16)
    low, high = student[:half, :], student[half:, :]
    for i in range(packed.shape[0]):
        packed[i, :, :s_width] = low
        packed[i, :, s_width : 2 * s_width] = high
        packed[i, :, 2 * s_width :] = chosen


def choose_kernel(half, s_width, source, gains, everyone, piece):
    count = everyone.shape[0]
    t_width = everyone.shape[1] - 2 * s_width
    wide = lax.axis_index("tensor_0") * lax.axis_size("tensor_1") + lax.axis_index("tensor_1")
    j = lax.broadcasted_iota(jnp.int32, (count, count), 1)
    low = (j // half) * (2 * half) + j % half
    want = jnp.broadcast_to(source[:, :1], (count, count))
    one = lambda hit: jnp.where(hit, 1.0, 0.0).astype(jnp.bfloat16)
    dot = functools.partial(jnp.dot, preferred_element_type=jnp.float32)
    chosen = dot(one(want == low), everyone[:, :s_width])
    chosen += dot(one(want == low + half), everyone[:, s_width : 2 * s_width])
    piece[:, :s_width] = chosen.astype(jnp.bfloat16)
    values = everyone[:, 2 * s_width :].astype(jnp.float32)
    piece[:, s_width : s_width + t_width] = (values * gains[pl.ds(wide, 1), :]).astype(jnp.bfloat16)
    rest = jnp.sum(values * values, axis=1, keepdims=True)
    at = s_width + t_width
    for k in range(TERMS):
        term = rest.astype(jnp.bfloat16)
        piece[:, at + k : at + k + 1] = term
        rest = rest - term.astype(jnp.float32)


def block_kernel(offsets, had, t_width, s_width, *refs):
    n = len(offsets)
    blocks, refs = refs[:n], refs[n:]
    t_head, s_head, t_twin, s_twin = refs[:4]
    refs = refs[4:]
    if had:
        before, refs = refs[:2], refs[2:]
    mine, sent, t_own_buf, s_own_buf, t_twin_buf, s_twin_buf, sems = refs
    y, core = lax.axis_index("tensor_0"), lax.axis_index("tensor_1")
    ys, cores = lax.axis_size("tensor_0"), lax.axis_size("tensor_1")
    vocab = t_head.shape[1]
    copies = []
    for i, offset in enumerate(offsets):
        at = lax.rem(y + (offset % ys), ys)
        wide = at * cores + core
        froms = (
            t_head.at[pl.ds(pl.multiple_of(wide * t_width, 64), t_width), :],
            s_head.at[pl.ds(pl.multiple_of(wide * s_width, 64), s_width), :],
            t_twin.at[at],
            s_twin.at[at],
        )
        tos = (t_own_buf.at[i], s_own_buf.at[i], t_twin_buf.at[i], s_twin_buf.at[i])
        for k in range(4):
            copy = pltpu.make_async_copy(froms[k], tos[k], sems.at[i, k])
            copy.start()
            copies.append(copy)
    t_mine = s_mine = t_sent = s_sent = squares = None
    dot = functools.partial(jnp.dot, preferred_element_type=jnp.float32)
    if had:
        t_mine, s_mine = before[0][:, :vocab], before[0][:, vocab:]
        t_sent, s_sent = before[1][:, :vocab], before[1][:, vocab : 2 * vocab]
        squares = before[1][:, 2 * vocab : 2 * vocab + 1]
    plus = lambda total, term: term if total is None else total + term
    for i in range(n):
        for k in range(4):
            copies[4 * i + k].wait()
        at = s_width + t_width
        for k in range(TERMS):
            squares = plus(squares, blocks[i][:, at + k : at + k + 1].astype(jnp.float32))
        student, scaled = blocks[i][:, :s_width], blocks[i][:, s_width:at]
        t_mine = plus(t_mine, dot(scaled, t_own_buf[i]))
        t_sent = plus(t_sent, dot(scaled, t_twin_buf[i]))
        s_mine = plus(s_mine, dot(student, s_own_buf[i]))
        s_sent = plus(s_sent, dot(student, s_twin_buf[i]))
    mine[:, :vocab], mine[:, vocab:] = t_mine, s_mine
    sent[:, :vocab], sent[:, vocab : 2 * vocab] = t_sent, s_sent
    sent[:, 2 * vocab :] = jnp.broadcast_to(squares, (squares.shape[0], 128))


def block_products(found, heads, before):
    offsets, blocks = [f[0] for f in found], [f[1] for f in found]
    n, rows, vocab = len(found), blocks[0].shape[0], heads[0].shape[1]
    t_width, s_width = heads[2].shape[1], heads[3].shape[1]
    had = before is not None
    bf16 = jnp.bfloat16
    return pl.pallas_call(
        functools.partial(block_kernel, offsets, had, t_width, s_width),
        out_shape=(
            jax.ShapeDtypeStruct((rows, 2 * vocab), jnp.float32),
            jax.ShapeDtypeStruct((rows, 2 * vocab + 128), jnp.float32),
        ),
        in_specs=[VMEM] * n + [ANY] * 4 + [VMEM] * (2 if had else 0),
        out_specs=(VMEM, VMEM),
        scratch_shapes=[
            pltpu.VMEM((n, t_width, vocab), bf16),
            pltpu.VMEM((n, s_width, vocab), bf16),
            pltpu.VMEM((n, t_width, vocab), bf16),
            pltpu.VMEM((n, s_width, vocab), bf16),
            pltpu.SemaphoreType.DMA((n, 4)),
        ],
        compiler_params=pltpu.CompilerParams(vmem_limit_bytes=48 << 20),
        cost_estimate=pl.CostEstimate(
            flops=4 * n * rows * vocab * (t_width + s_width),
            bytes_accessed=4 * n * vocab * (t_width + s_width),
            transcendentals=0,
        ),
    )(*blocks, *heads, *(before if had else ()))


def merge(parts):
    teacher, student, mean, picked = (parts[:, k] for k in range(4))
    top_t, top_s = jnp.max(teacher, axis=0), jnp.max(student, axis=0)
    sum_t = jnp.sum(jnp.exp(teacher - top_t), axis=0)
    weight = jnp.exp(student - top_s)
    sum_s = jnp.sum(weight, axis=0)
    mean = jnp.sum(weight * mean, axis=0) / sum_s
    return jnp.stack([top_t + jnp.log(sum_t), top_s + jnp.log(sum_s), mean, jnp.sum(picked, axis=0)])


def on_device(
    teacher_hidden,
    student_hidden,
    teacher_head,
    student_head,
    teacher_gain,
    lengths,
    student_row,
    targets,
):
    dp_count = lax.axis_size(DP)
    tensor_count = lax.axis_size(TENSOR)
    y_count, core_count = (lax.axis_size(a) for a in TENSOR)
    local_tokens, t_width = teacher_hidden.shape
    s_width = student_hidden.shape[1]
    token_count = local_tokens * dp_count
    vocab_local = teacher_head.shape[1]
    dp_index = lax.axis_index(DP)
    core = lax.axis_index("tensor_1")
    vocab_start = (dp_index * tensor_count + lax.axis_index(TENSOR)) * vocab_local

    first, second = lengths.reshape(dp_count, 2)[:, :1], lengths.reshape(dp_count, 2)[:, 1:]
    slot = jnp.arange(LIVE_DEV, dtype=jnp.int32)[None, :]
    place = jnp.where(slot < first, slot, SLOT + slot - first)
    live = slot < first + second
    group = jnp.arange(dp_count, dtype=jnp.int32)[:, None] * local_tokens
    row_token = jnp.where(live, group + place, -1).reshape(-1)
    row_live = live.reshape(-1).astype(jnp.float32)
    rows = row_token.shape[0]

    half = local_tokens // 2
    packed = pl.pallas_call(
        pack_kernel,
        out_shape=jax.ShapeDtypeStruct((dp_count, half, 2 * s_width + t_width), jnp.bfloat16),
        in_specs=[SMEM, VMEM, VMEM],
        out_specs=VMEM,
        compiler_params=pltpu.CompilerParams(vmem_limit_bytes=62 << 20),
    )(lengths, teacher_hidden, student_hidden)
    t_blocks = teacher_head.reshape(y_count, core_count, t_width, vocab_local)
    s_blocks = student_head.reshape(y_count, core_count, s_width, vocab_local)
    other = lambda blocks: lax.dynamic_index_in_dim(blocks, 1 - core, 1, keepdims=False)
    twins = [shifted(other(blocks), "tensor_1", 1) for blocks in (t_blocks, s_blocks)]
    heads = (teacher_head, student_head, *twins)
    gains = teacher_gain.reshape(tensor_count, t_width)
    everyone = lax.all_to_all(packed, DP, 0, 0)

    token_of = row_token[:, None] == jnp.arange(token_count, dtype=jnp.int32)[None, :]
    row_source = jnp.sum(jnp.where(token_of, student_row[None, :], 0), axis=1)
    row_target = jnp.sum(jnp.where(token_of, targets[None, :], 0), axis=1)
    piece = pl.pallas_call(
        functools.partial(choose_kernel, half, s_width),
        out_shape=jax.ShapeDtypeStruct((rows, s_width + t_width + TERMS), jnp.bfloat16),
        in_specs=[VMEM] * 3,
        out_specs=VMEM,
        compiler_params=pltpu.CompilerParams(vmem_limit_bytes=8 << 20),
    )(jnp.broadcast_to(row_source[:, None], (rows, 128)), gains, everyone.reshape(rows, -1))

    found = ring_pieces(piece, "tensor_0")
    parts = block_products(found[:3], heads, None)
    parts = block_products(found[3:-1], heads, parts)
    mine, sent = block_products(found[-1:], heads, parts)
    squares = sent[:, 2 * vocab_local :][:, :1]
    got = shifted(sent, "tensor_1", 1)
    mean_square = (squares + got[:, 2 * vocab_local :][:, :1]) / (t_width * tensor_count)
    row_scale = lax.rsqrt(mean_square + 1e-06)
    both = mine + got[:, : 2 * vocab_local]
    teacher_logits = both[:, :vocab_local] * row_scale
    student_logits = both[:, vocab_local:]

    gap = student_logits - teacher_logits
    hits = (row_target - vocab_start)[:, None] == jnp.arange(vocab_local, dtype=jnp.int32)[None, :]
    picked = jnp.sum(jnp.where(hits, gap, 0.0), axis=1)
    teacher_max = jnp.max(teacher_logits, axis=1)
    student_max = jnp.max(student_logits, axis=1)
    teacher_sum = jnp.sum(jnp.exp(teacher_logits - teacher_max[:, None]), axis=1)
    student_exp = jnp.exp(student_logits - student_max[:, None])
    student_sum = jnp.sum(student_exp, axis=1)
    mean = jnp.sum(student_exp * gap, axis=1) / student_sum
    local = jnp.stack(
        [teacher_max + jnp.log(teacher_sum), student_max + jnp.log(student_sum), mean, picked]
    )
    merged = merge(spread(merge(spread(local, DP)), TENSOR))
    teacher_lse, student_lse, mean, picked = (merged[k] for k in range(4))

    student_prob = jnp.exp(student_logits - student_lse[:, None])
    gradient = (row_live[:, None] * student_prob * (gap - mean[:, None])).astype(jnp.bfloat16)
    lse_gap = teacher_lse - student_lse
    token_ids = jnp.arange(token_count, dtype=jnp.int32)
    unpack = (token_ids[:, None] == row_token[None, :]).astype(jnp.bfloat16)
    grad_logits = jnp.dot(unpack, gradient, preferred_element_type=jnp.float32).astype(jnp.bfloat16)
    own_ids = dp_index * local_tokens + jnp.arange(local_tokens, dtype=jnp.int32)
    own_of = own_ids[:, None] == row_token[None, :]
    divergence = jnp.sum(jnp.where(own_of, (mean + lse_gap)[None, :], 0.0), axis=1)
    log_ratio = jnp.sum(jnp.where(own_of, (picked + lse_gap)[None, :], 0.0), axis=1)
    return (grad_logits, divergence, log_ratio)


def solution(mesh):
    finer = Mesh(mesh.devices.reshape(8, 4, 8, 2), ("dp_0", "dp_1", "tensor_0", "tensor_1"))
    in_specs = (
        P(DP, TENSOR),
        P(DP, TENSOR),
        P(None, DP_TENSOR),
        P(None, DP_TENSOR),
        P(),
        P(),
        P(),
        P(),
    )
    out_specs = (P(None, DP_TENSOR), P(DP), P(DP))
    return jax.shard_map(
        on_device, mesh=finer, in_specs=in_specs, out_specs=out_specs, check_vma=False
    )
```

```python
import functools
import math

import jax
import jax.numpy as jnp
import numpy as np
from jax import lax
from jax.experimental import pallas as pl
from jax.experimental.pallas import tpu as pltpu
from jax.sharding import Mesh
from jax.sharding import PartitionSpec as P


SLOT = 8
LIVE_DEV = 8
DP = ("dp_0", "dp_1")
TENSOR = ("tensor_0", "tensor_1")
DP_TENSOR = ("dp_0", "dp_1", "tensor_0", "tensor_1")


def spread(array, axes):
    count = lax.axis_size(axes)
    return lax.all_to_all(jnp.broadcast_to(array, (count, *array.shape)), axes, 0, 0)


def shifted(array, axis, by):
    count = lax.axis_size(axis)
    return lax.ppermute(array, axis, [(i, (i + by) % count) for i in range(count)])


def ids_of(axes):
    return np.arange(math.prod(lax.axis_size(a) for a in axes)).reshape([lax.axis_size(a) for a in axes])


def stepped(array, by):
    ids = ids_of(DP_TENSOR)
    after = ids.copy()
    after[..., 0] = np.roll(ids[..., 0], -by, axis=2)
    after[..., 1] = np.roll(ids[..., 1], -by, axis=0)
    perm = list(zip(ids.reshape(-1).tolist(), after.reshape(-1).tolist()))
    return lax.ppermute(array, DP_TENSOR, perm)


def plane_groups():
    ids = ids_of(DP_TENSOR)
    zero = ids[..., 0].transpose(2, 0, 1).reshape(ids.shape[2], -1)
    one = ids[..., 1].transpose(0, 2, 1).reshape(ids.shape[0], -1)
    return np.concatenate([zero, one]).tolist()


def ring_pieces(piece, count):
    found = [(0, piece)]
    ahead = behind = piece
    for k in range(1, count // 2):
        ahead = stepped(ahead, 1)
        behind = stepped(behind, -1)
        found += [(-k, ahead), (k, behind)]
    return found + [(-(count // 2), stepped(ahead, 1))]


VMEM = pl.BlockSpec(memory_space=pltpu.VMEM)
SMEM = pl.BlockSpec(memory_space=pltpu.SMEM)


def pick_kernel(lengths, teacher, student, keep, give):
    group = lax.axis_index("dp_0") * lax.axis_size("dp_1") + lax.axis_index("dp_1")
    first, second = lengths[2 * group], lengths[2 * group + 1]
    half, s_width, t_width = student.shape[0] // 2, student.shape[1], teacher.shape[1]
    grid = (LIVE_DEV, teacher.shape[0])
    slot, row = (lax.broadcasted_iota(jnp.int32, grid, d) for d in range(2))
    place = jnp.where(slot < first, slot, SLOT + slot - first)
    pick = jnp.where((place == row) & (slot < first + second), 1.0, 0.0)
    chosen = jnp.dot(
        pick.astype(jnp.bfloat16), teacher[...], preferred_element_type=jnp.float32
    ).astype(jnp.bfloat16)

    def write(students, teachers):
        students[:, :s_width] = student[:half, :]
        students[:, s_width:] = student[half:, :]
        teachers[...] = jnp.zeros(teachers.shape, teachers.dtype)
        teachers[:, :t_width] = chosen

    core = lax.axis_index("tensor_1")
    pl.when(core == 0)(lambda: write(keep, give))
    pl.when(core == 1)(lambda: write(give, keep))


def pack_kernel(s_width, t_width, keep, got, packed):
    core = lax.axis_index("tensor_1")

    @pl.when(core == 0)
    def _():
        for i in range(packed.shape[0]):
            for k, part in enumerate((keep, got)):
                packed[i, :, k * s_width : (k + 1) * s_width] = part[:, :s_width]
                packed[i, :, (2 + k) * s_width : (3 + k) * s_width] = part[:, s_width:]

    @pl.when(core == 1)
    def _():
        for i in range(packed.shape[0]):
            packed[i, :, :t_width] = got[:, :t_width]
            packed[i, :, t_width : 2 * t_width] = keep[:, :t_width]
            packed[i, :, 2 * t_width :] = jnp.zeros(
                (packed.shape[1], packed.shape[2] - 2 * t_width), packed.dtype
            )


def choose_kernel(half, source, gain, everyone, piece, gains):
    count, width = everyone.shape
    s_wide = width // 2
    core = lax.axis_index("tensor_1")
    gains[...] = gain[...]

    @pl.when(core == 0)
    def _():
        j = lax.broadcasted_iota(jnp.int32, (count, count), 1)
        low = (j // half) * (2 * half) + j % half
        want = jnp.broadcast_to(source[:, :1], (count, count))
        one = lambda hit: jnp.where(hit, 1.0, 0.0).astype(jnp.bfloat16)
        dot = functools.partial(jnp.dot, preferred_element_type=jnp.float32)
        chosen = dot(one(want == low), everyone[:, :s_wide])
        chosen += dot(one(want == low + half), everyone[:, s_wide:])
        piece[:, :s_wide] = chosen.astype(jnp.bfloat16)
        piece[:, s_wide:] = jnp.zeros((count, piece.shape[1] - s_wide), piece.dtype)

    @pl.when(core == 1)
    def _():
        piece[...] = everyone[:, : piece.shape[1]]


def block_kernel(offsets, had, s_wide, *refs):
    n = len(offsets)
    blocks, (gains, own, twin), refs = refs[:n], refs[n : n + 3], refs[n + 3 :]
    before, (keep, give, own_buf, twin_buf, sems) = (refs[:2] if had else ()), refs[-5:]
    bufs = (own_buf, twin_buf)

    def fetch(starts, size):
        copies = []
        for i, start in enumerate(starts):
            at = pl.ds(start, size)
            copies.append(
                [
                    pltpu.make_async_copy(head.at[at, :], buf.at[at, :], sems.at[i, k])
                    for k, (head, buf) in enumerate(zip((own, twin), bufs))
                ]
            )
            for copy in copies[-1]:
                copy.start()
        return copies

    rows, t_wide = blocks[0].shape
    dot = functools.partial(jnp.dot, preferred_element_type=jnp.float32)
    core = lax.axis_index("tensor_1")

    @pl.when(core == 0)
    def _():
        y, ys = lax.axis_index("tensor_0"), lax.axis_size("tensor_0")
        totals = [ref[...] for ref in before] if had else [0.0, 0.0]
        starts = [
            pl.multiple_of(lax.rem(y + offset % ys, ys) * s_wide, s_wide) for offset in offsets
        ]
        for block, start, copies in zip(blocks, starts, fetch(starts, s_wide)):
            for copy in copies:
                copy.wait()
            student, features = block[:, :s_wide], pl.ds(start, s_wide)
            totals = [total + dot(student, buf[features, :]) for total, buf in zip(totals, bufs)]
        keep[...], give[...] = totals

    @pl.when(core == 1)
    def _():
        z, zs = lax.axis_index("dp_0"), lax.axis_size("dp_0")
        for k, ref in enumerate((keep, give)):
            ref[...] = before[k][...] if had else jnp.zeros(ref.shape, ref.dtype)
        ys = lax.axis_size("tensor_0")
        copies = fetch([k * t_wide for k in range(ys)], t_wide)
        count = rows // ys
        part = lambda k: jnp.concatenate(
            [block[k * count : (k + 1) * count, :] for block in blocks], axis=0
        ).astype(jnp.float32)
        squares = 0.0
        for k in range(ys):
            values = part(k)
            squares += jnp.sum(values * values, axis=1, keepdims=True)
        row_scale = lax.rsqrt(squares / (ys * t_wide) + 1e-06)
        totals = [0.0, 0.0]
        for k in range(ys):
            normed = (part(k) * row_scale * gains[k : k + 1, :]).astype(jnp.bfloat16)
            for copy in copies[k]:
                copy.wait()
            features = slice(k * t_wide, (k + 1) * t_wide)
            totals = [total + dot(normed, buf[features, :]) for total, buf in zip(totals, bufs)]
        for i, offset in enumerate(offsets):
            at = pl.multiple_of(lax.rem(z + offset % zs, zs) * count, count)
            for ref, total in zip((keep, give), totals):
                ref[pl.ds(at, count), :] = total[i * count : (i + 1) * count, :]


def block_products(found, gains, heads, s_wide, before):
    offsets, blocks = [f[0] for f in found], [f[1] for f in found]
    rows, vocab = blocks[0].shape[0], heads[0].shape[1]
    shape = jax.ShapeDtypeStruct((rows, vocab), jnp.float32)
    return pl.pallas_call(
        functools.partial(block_kernel, offsets, bool(before), s_wide),
        out_shape=(shape, shape),
        in_specs=[VMEM] * (len(blocks) + 1) + [ANY, ANY] + [VMEM] * len(before),
        out_specs=(VMEM, VMEM),
        scratch_shapes=[
            pltpu.VMEM(heads[0].shape, jnp.bfloat16),
            pltpu.VMEM(heads[0].shape, jnp.bfloat16),
            pltpu.SemaphoreType.DMA((lax.axis_size("tensor_0"), 2)),
        ],
        compiler_params=pltpu.CompilerParams(vmem_limit_bytes=LIMIT),
        cost_estimate=pl.CostEstimate(
            flops=4 * len(blocks) * rows * vocab * s_wide,
            bytes_accessed=4 * len(blocks) * vocab * s_wide,
            transcendentals=0,
        ),
    )(*blocks, gains, *heads, *before)


LIMIT = 48 << 20
ANY = pl.BlockSpec(memory_space=pl.ANY)


def merge(parts):
    teacher, student, mean, picked = (parts[:, k] for k in range(4))
    top_t, top_s = jnp.max(teacher, axis=0), jnp.max(student, axis=0)
    sum_t = jnp.sum(jnp.exp(teacher - top_t), axis=0)
    weight = jnp.exp(student - top_s)
    sum_s = jnp.sum(weight, axis=0)
    mean = jnp.sum(weight * mean, axis=0) / sum_s
    return jnp.stack([top_t + jnp.log(sum_t), top_s + jnp.log(sum_s), mean, jnp.sum(picked, axis=0)])


def on_device(
    teacher_hidden,
    student_hidden,
    teacher_head,
    student_head,
    teacher_gain,
    lengths,
    student_row,
    targets,
):
    dp_count = lax.axis_size(DP)
    tensor_count = lax.axis_size(TENSOR)
    y_count, core_count = (lax.axis_size(a) for a in TENSOR)
    local_tokens, t_width = teacher_hidden.shape
    s_width = student_hidden.shape[1]
    token_count = local_tokens * dp_count
    vocab_local = teacher_head.shape[1]
    dp_index = lax.axis_index(DP)
    core = lax.axis_index("tensor_1")
    vocab_start = (dp_index * tensor_count + lax.axis_index(TENSOR)) * vocab_local

    first, second = lengths.reshape(dp_count, 2)[:, :1], lengths.reshape(dp_count, 2)[:, 1:]
    slot = jnp.arange(LIVE_DEV, dtype=jnp.int32)[None, :]
    place = jnp.where(slot < first, slot, SLOT + slot - first)
    live = slot < first + second
    group = jnp.arange(dp_count, dtype=jnp.int32)[:, None] * local_tokens
    row_token = jnp.where(live, group + place, -1).reshape(-1)
    row_live = live.reshape(-1).astype(jnp.float32)
    rows = row_token.shape[0]

    half = local_tokens // 2
    s_wide, t_wide = s_width * core_count, t_width * core_count
    pair = jax.ShapeDtypeStruct((half, 2 * s_width), jnp.bfloat16)
    small = pltpu.CompilerParams(vmem_limit_bytes=8 << 20)
    keep, give = pl.pallas_call(
        pick_kernel,
        out_shape=(pair, pair),
        in_specs=[SMEM, VMEM, VMEM],
        out_specs=(VMEM, VMEM),
        compiler_params=pltpu.CompilerParams(vmem_limit_bytes=62 << 20),
    )(lengths, teacher_hidden, student_hidden)
    packed = pl.pallas_call(
        functools.partial(pack_kernel, s_width, t_width),
        out_shape=jax.ShapeDtypeStruct((dp_count, half, 2 * s_wide), jnp.bfloat16),
        in_specs=[VMEM, VMEM],
        out_specs=VMEM,
        compiler_params=pltpu.CompilerParams(vmem_limit_bytes=62 << 20),
    )(keep, shifted(give, "tensor_1", 1))
    everyone = lax.all_to_all(packed, DP_TENSOR, 0, 0, axis_index_groups=plane_groups())
    tall = jnp.pad(student_head, ((0, t_wide * y_count - s_wide * y_count), (0, 0)))
    away = jnp.where(core == 0, teacher_head, tall)
    own = jnp.where(core == 0, tall, teacher_head)
    heads = (own, shifted(away, "tensor_1", 1))
    gains = teacher_gain.reshape(y_count, t_wide)

    token_of = row_token[:, None] == jnp.arange(token_count, dtype=jnp.int32)[None, :]
    row_source = jnp.sum(jnp.where(token_of, student_row[None, :], 0), axis=1)
    row_target = jnp.sum(jnp.where(token_of, targets[None, :], 0), axis=1)
    piece, gains = pl.pallas_call(
        functools.partial(choose_kernel, half),
        out_shape=(
            jax.ShapeDtypeStruct((rows, t_wide), jnp.bfloat16),
            jax.ShapeDtypeStruct(gains.shape, jnp.float32),
        ),
        in_specs=[VMEM] * 3,
        out_specs=(VMEM, VMEM),
        compiler_params=small,
    )(jnp.broadcast_to(row_source[:, None], (rows, 128)), gains, everyone.reshape(rows, -1))

    found = ring_pieces(piece, y_count)
    parts = block_products(found[:3], gains, heads, s_wide, ())
    parts = block_products(found[3:-1], gains, heads, s_wide, parts)
    kept, sent = block_products(found[-1:], gains, heads, s_wide, parts)
    got = shifted(sent, "tensor_1", 1)
    student_logits = jnp.where(core == 0, kept, got)
    teacher_logits = jnp.where(core == 0, got, kept)

    gap = student_logits - teacher_logits
    hits = (row_target - vocab_start)[:, None] == jnp.arange(vocab_local, dtype=jnp.int32)[None, :]
    picked = jnp.sum(jnp.where(hits, gap, 0.0), axis=1)
    teacher_max = jnp.max(teacher_logits, axis=1)
    student_max = jnp.max(student_logits, axis=1)
    teacher_sum = jnp.sum(jnp.exp(teacher_logits - teacher_max[:, None]), axis=1)
    student_exp = jnp.exp(student_logits - student_max[:, None])
    student_sum = jnp.sum(student_exp, axis=1)
    mean = jnp.sum(student_exp * gap, axis=1) / student_sum
    local = jnp.stack(
        [teacher_max + jnp.log(teacher_sum), student_max + jnp.log(student_sum), mean, picked]
    )
    merged = merge(spread(merge(spread(local, DP)), TENSOR))
    teacher_lse, student_lse, mean, picked = (merged[k] for k in range(4))

    student_prob = jnp.exp(student_logits - student_lse[:, None])
    gradient = (row_live[:, None] * student_prob * (gap - mean[:, None])).astype(jnp.bfloat16)
    lse_gap = teacher_lse - student_lse
    token_ids = jnp.arange(token_count, dtype=jnp.int32)
    unpack = (token_ids[:, None] == row_token[None, :]).astype(jnp.bfloat16)
    grad_logits = jnp.dot(unpack, gradient, preferred_element_type=jnp.float32).astype(jnp.bfloat16)
    own_ids = dp_index * local_tokens + jnp.arange(local_tokens, dtype=jnp.int32)
    own_of = own_ids[:, None] == row_token[None, :]
    divergence = jnp.sum(jnp.where(own_of, (mean + lse_gap)[None, :], 0.0), axis=1)
    log_ratio = jnp.sum(jnp.where(own_of, (picked + lse_gap)[None, :], 0.0), axis=1)
    return (grad_logits, divergence, log_ratio)


def solution(mesh):
    finer = Mesh(mesh.devices.reshape(8, 4, 8, 2), ("dp_0", "dp_1", "tensor_0", "tensor_1"))
    in_specs = (
        P(DP, TENSOR),
        P(DP, TENSOR),
        P(None, DP_TENSOR),
        P(None, DP_TENSOR),
        P(),
        P(),
        P(),
        P(),
    )
    out_specs = (P(None, DP_TENSOR), P(DP), P(DP))
    return jax.shard_map(
        on_device, mesh=finer, in_specs=in_specs, out_specs=out_specs, check_vma=False
    )
```

```python
import functools
import math

import jax
import jax.numpy as jnp
import numpy as np
from jax import lax
from jax.experimental import pallas as pl
from jax.experimental.pallas import tpu as pltpu
from jax.sharding import Mesh
from jax.sharding import PartitionSpec as P


SLOT = 8
LIVE_DEV = 8
DP = ("dp_0", "dp_1")
TENSOR = ("tensor_0", "tensor_1")
DP_TENSOR = ("dp_0", "dp_1", "tensor_0", "tensor_1")


def spread(array, axes):
    count = lax.axis_size(axes)
    return lax.all_to_all(jnp.broadcast_to(array, (count, *array.shape)), axes, 0, 0)


def shifted(array, axis, by):
    count = lax.axis_size(axis)
    return lax.ppermute(array, axis, [(i, (i + by) % count) for i in range(count)])


def ids_of(axes):
    return np.arange(math.prod(lax.axis_size(a) for a in axes)).reshape([lax.axis_size(a) for a in axes])


def stepped(array, by):
    ids = ids_of(DP_TENSOR)
    after = ids.copy()
    after[..., 0] = np.roll(ids[..., 0], -by, axis=2)
    after[..., 1] = np.roll(ids[..., 1], -by, axis=0)
    perm = list(zip(ids.reshape(-1).tolist(), after.reshape(-1).tolist()))
    return lax.ppermute(array, DP_TENSOR, perm)


def plane_groups():
    ids = ids_of(DP_TENSOR)
    zero = ids[..., 0].transpose(2, 0, 1).reshape(ids.shape[2], -1)
    one = ids[..., 1].transpose(0, 2, 1).reshape(ids.shape[0], -1)
    return np.concatenate([zero, one]).tolist()


def ring_pieces(piece):
    ahead_2, behind_2 = stepped(piece, 2), stepped(piece, -2)
    ahead_1, behind_1 = stepped(piece, 1), stepped(piece, -1)
    ahead_3, across, behind_3 = stepped(ahead_2, 1), stepped(ahead_2, 2), stepped(behind_2, -1)
    return [
        (0, piece),
        (-1, ahead_1),
        (1, behind_1),
        (-2, ahead_2),
        (2, behind_2),
        (-3, ahead_3),
        (3, behind_3),
        (-4, across),
    ]


VMEM = pl.BlockSpec(memory_space=pltpu.VMEM)
SMEM = pl.BlockSpec(memory_space=pltpu.SMEM)


def pick_kernel(lengths, teacher, student, keep, give):
    group = lax.axis_index("dp_0") * lax.axis_size("dp_1") + lax.axis_index("dp_1")
    first, second = lengths[2 * group], lengths[2 * group + 1]
    half, s_width, t_width = student.shape[0] // 2, student.shape[1], teacher.shape[1]
    grid = (LIVE_DEV, teacher.shape[0])
    slot, row = (lax.broadcasted_iota(jnp.int32, grid, d) for d in range(2))
    place = jnp.where(slot < first, slot, SLOT + slot - first)
    pick = jnp.where((place == row) & (slot < first + second), 1.0, 0.0)
    chosen = jnp.dot(
        pick.astype(jnp.bfloat16), teacher[...], preferred_element_type=jnp.float32
    ).astype(jnp.bfloat16)

    def write(students, teachers):
        students[:, :s_width] = student[:half, :]
        students[:, s_width:] = student[half:, :]
        teachers[...] = jnp.zeros(teachers.shape, teachers.dtype)
        teachers[:, :t_width] = chosen

    core = lax.axis_index("tensor_1")
    pl.when(core == 0)(lambda: write(keep, give))
    pl.when(core == 1)(lambda: write(give, keep))


def pack_kernel(s_width, t_width, keep, got, packed):
    core = lax.axis_index("tensor_1")

    @pl.when(core == 0)
    def _():
        for i in range(packed.shape[0]):
            for k, part in enumerate((keep, got)):
                packed[i, :, k * s_width : (k + 1) * s_width] = part[:, :s_width]
                packed[i, :, (2 + k) * s_width : (3 + k) * s_width] = part[:, s_width:]

    @pl.when(core == 1)
    def _():
        for i in range(packed.shape[0]):
            packed[i, :, :t_width] = got[:, :t_width]
            packed[i, :, t_width : 2 * t_width] = keep[:, :t_width]
            packed[i, :, 2 * t_width :] = jnp.zeros(
                (packed.shape[1], packed.shape[2] - 2 * t_width), packed.dtype
            )


def choose_kernel(half, source, gain, everyone, piece, gains):
    count, width = everyone.shape
    s_wide = width // 2
    core = lax.axis_index("tensor_1")
    gains[...] = gain[...]

    @pl.when(core == 0)
    def _():
        j = lax.broadcasted_iota(jnp.int32, (count, count), 1)
        low = (j // half) * (2 * half) + j % half
        want = jnp.broadcast_to(source[:, :1], (count, count))
        one = lambda hit: jnp.where(hit, 1.0, 0.0).astype(jnp.bfloat16)
        dot = functools.partial(jnp.dot, preferred_element_type=jnp.float32)
        chosen = dot(one(want == low), everyone[:, :s_wide])
        chosen += dot(one(want == low + half), everyone[:, s_wide:])
        piece[:, :s_wide] = chosen.astype(jnp.bfloat16)
        piece[:, s_wide:] = jnp.zeros((count, piece.shape[1] - s_wide), piece.dtype)

    @pl.when(core == 1)
    def _():
        piece[...] = everyone[:, : piece.shape[1]]


def block_kernel(offsets, had, s_wide, *refs):
    n = len(offsets)
    blocks, (gains, own, twin), refs = refs[:n], refs[n : n + 3], refs[n + 3 :]
    before, (keep, give, own_buf, twin_buf, sems) = (refs[:2] if had else ()), refs[-5:]
    bufs = (own_buf, twin_buf)

    def fetch(starts, size):
        copies = []
        for i, start in enumerate(starts):
            at = pl.ds(start, size)
            copies.append(
                [
                    pltpu.make_async_copy(head.at[at, :], buf.at[at, :], sems.at[i, k])
                    for k, (head, buf) in enumerate(zip((own, twin), bufs))
                ]
            )
            for copy in copies[-1]:
                copy.start()
        return copies

    rows, t_wide = blocks[0].shape
    dot = functools.partial(jnp.dot, preferred_element_type=jnp.float32)
    core = lax.axis_index("tensor_1")

    @pl.when(core == 0)
    def _():
        y, ys = lax.axis_index("tensor_0"), lax.axis_size("tensor_0")
        totals = [ref[...] for ref in before] if had else [0.0, 0.0]
        starts = [
            pl.multiple_of(lax.rem(y + offset % ys, ys) * s_wide, s_wide) for offset in offsets
        ]
        for block, start, copies in zip(blocks, starts, fetch(starts, s_wide)):
            for copy in copies:
                copy.wait()
            student, features = block[:, :s_wide], pl.ds(start, s_wide)
            totals = [total + dot(student, buf[features, :]) for total, buf in zip(totals, bufs)]
        keep[...], give[...] = totals

    @pl.when(core == 1)
    def _():
        z, zs = lax.axis_index("dp_0"), lax.axis_size("dp_0")
        for k, ref in enumerate((keep, give)):
            ref[...] = before[k][...] if had else jnp.zeros(ref.shape, ref.dtype)
        ys = lax.axis_size("tensor_0")
        copies = fetch([k * t_wide for k in range(ys)], t_wide)
        count = rows // ys
        part = lambda k: jnp.concatenate(
            [block[k * count : (k + 1) * count, :] for block in blocks], axis=0
        ).astype(jnp.float32)
        squares = 0.0
        for k in range(ys):
            values = part(k)
            squares += jnp.sum(values * values, axis=1, keepdims=True)
        row_scale = lax.rsqrt(squares / (ys * t_wide) + 1e-06)
        totals = [0.0, 0.0]
        for k in range(ys):
            normed = (part(k) * row_scale * gains[k : k + 1, :]).astype(jnp.bfloat16)
            for copy in copies[k]:
                copy.wait()
            features = slice(k * t_wide, (k + 1) * t_wide)
            totals = [total + dot(normed, buf[features, :]) for total, buf in zip(totals, bufs)]
        for i, offset in enumerate(offsets):
            at = pl.multiple_of(lax.rem(z + offset % zs, zs) * count, count)
            for ref, total in zip((keep, give), totals):
                ref[pl.ds(at, count), :] = total[i * count : (i + 1) * count, :]


def block_products(found, gains, heads, s_wide, before):
    offsets, blocks = [f[0] for f in found], [f[1] for f in found]
    rows, vocab = blocks[0].shape[0], heads[0].shape[1]
    shape = jax.ShapeDtypeStruct((rows, vocab), jnp.float32)
    return pl.pallas_call(
        functools.partial(block_kernel, offsets, bool(before), s_wide),
        out_shape=(shape, shape),
        in_specs=[VMEM] * (len(blocks) + 1) + [ANY, ANY] + [VMEM] * len(before),
        out_specs=(VMEM, VMEM),
        scratch_shapes=[
            pltpu.VMEM(heads[0].shape, jnp.bfloat16),
            pltpu.VMEM(heads[0].shape, jnp.bfloat16),
            pltpu.SemaphoreType.DMA((lax.axis_size("tensor_0"), 2)),
        ],
        compiler_params=pltpu.CompilerParams(vmem_limit_bytes=LIMIT),
        cost_estimate=pl.CostEstimate(
            flops=4 * len(blocks) * rows * vocab * s_wide,
            bytes_accessed=4 * len(blocks) * vocab * s_wide,
            transcendentals=0,
        ),
    )(*blocks, gains, *heads, *before)


LIMIT = 48 << 20
ANY = pl.BlockSpec(memory_space=pl.ANY)


def merge(parts):
    teacher, student, mean, picked = (parts[:, k] for k in range(4))
    top_t, top_s = jnp.max(teacher, axis=0), jnp.max(student, axis=0)
    sum_t = jnp.sum(jnp.exp(teacher - top_t), axis=0)
    weight = jnp.exp(student - top_s)
    sum_s = jnp.sum(weight, axis=0)
    mean = jnp.sum(weight * mean, axis=0) / sum_s
    return jnp.stack([top_t + jnp.log(sum_t), top_s + jnp.log(sum_s), mean, jnp.sum(picked, axis=0)])


def on_device(
    teacher_hidden,
    student_hidden,
    teacher_head,
    student_head,
    teacher_gain,
    lengths,
    student_row,
    targets,
):
    dp_count = lax.axis_size(DP)
    tensor_count = lax.axis_size(TENSOR)
    y_count, core_count = (lax.axis_size(a) for a in TENSOR)
    local_tokens, t_width = teacher_hidden.shape
    s_width = student_hidden.shape[1]
    token_count = local_tokens * dp_count
    vocab_local = teacher_head.shape[1]
    dp_index = lax.axis_index(DP)
    core = lax.axis_index("tensor_1")
    vocab_start = (dp_index * tensor_count + lax.axis_index(TENSOR)) * vocab_local

    first, second = lengths.reshape(dp_count, 2)[:, :1], lengths.reshape(dp_count, 2)[:, 1:]
    slot = jnp.arange(LIVE_DEV, dtype=jnp.int32)[None, :]
    place = jnp.where(slot < first, slot, SLOT + slot - first)
    live = slot < first + second
    group = jnp.arange(dp_count, dtype=jnp.int32)[:, None] * local_tokens
    row_token = jnp.where(live, group + place, -1).reshape(-1)
    row_live = live.reshape(-1).astype(jnp.float32)
    rows = row_token.shape[0]

    half = local_tokens // 2
    s_wide, t_wide = s_width * core_count, t_width * core_count
    pair = jax.ShapeDtypeStruct((half, 2 * s_width), jnp.bfloat16)
    small = pltpu.CompilerParams(vmem_limit_bytes=8 << 20)
    keep, give = pl.pallas_call(
        pick_kernel,
        out_shape=(pair, pair),
        in_specs=[SMEM, VMEM, VMEM],
        out_specs=(VMEM, VMEM),
        compiler_params=pltpu.CompilerParams(vmem_limit_bytes=62 << 20),
    )(lengths, teacher_hidden, student_hidden)
    packed = pl.pallas_call(
        functools.partial(pack_kernel, s_width, t_width),
        out_shape=jax.ShapeDtypeStruct((dp_count, half, 2 * s_wide), jnp.bfloat16),
        in_specs=[VMEM, VMEM],
        out_specs=VMEM,
        compiler_params=pltpu.CompilerParams(vmem_limit_bytes=62 << 20),
    )(keep, shifted(give, "tensor_1", 1))
    everyone = lax.all_to_all(packed, DP_TENSOR, 0, 0, axis_index_groups=plane_groups())
    tall = jnp.pad(student_head, ((0, t_wide * y_count - s_wide * y_count), (0, 0)))
    away = jnp.where(core == 0, teacher_head, tall)
    own = jnp.where(core == 0, tall, teacher_head)
    heads = (own, shifted(away, "tensor_1", 1))
    gains = teacher_gain.reshape(y_count, t_wide)

    token_of = row_token[:, None] == jnp.arange(token_count, dtype=jnp.int32)[None, :]
    row_source = jnp.sum(jnp.where(token_of, student_row[None, :], 0), axis=1)
    row_target = jnp.sum(jnp.where(token_of, targets[None, :], 0), axis=1)
    piece, gains = pl.pallas_call(
        functools.partial(choose_kernel, half),
        out_shape=(
            jax.ShapeDtypeStruct((rows, t_wide), jnp.bfloat16),
            jax.ShapeDtypeStruct(gains.shape, jnp.float32),
        ),
        in_specs=[VMEM] * 3,
        out_specs=(VMEM, VMEM),
        compiler_params=small,
    )(jnp.broadcast_to(row_source[:, None], (rows, 128)), gains, everyone.reshape(rows, -1))

    found = ring_pieces(piece)
    parts = block_products(found[:5], gains, heads, s_wide, ())
    kept, sent = block_products(found[5:], gains, heads, s_wide, parts)
    got = shifted(sent, "tensor_1", 1)
    student_logits = jnp.where(core == 0, kept, got)
    teacher_logits = jnp.where(core == 0, got, kept)

    gap = student_logits - teacher_logits
    hits = (row_target - vocab_start)[:, None] == jnp.arange(vocab_local, dtype=jnp.int32)[None, :]
    picked = jnp.sum(jnp.where(hits, gap, 0.0), axis=1)
    teacher_max = jnp.max(teacher_logits, axis=1)
    student_max = jnp.max(student_logits, axis=1)
    teacher_sum = jnp.sum(jnp.exp(teacher_logits - teacher_max[:, None]), axis=1)
    student_exp = jnp.exp(student_logits - student_max[:, None])
    student_sum = jnp.sum(student_exp, axis=1)
    mean = jnp.sum(student_exp * gap, axis=1) / student_sum
    local = jnp.stack(
        [teacher_max + jnp.log(teacher_sum), student_max + jnp.log(student_sum), mean, picked]
    )
    merged = merge(spread(merge(spread(local, DP)), TENSOR))
    teacher_lse, student_lse, mean, picked = (merged[k] for k in range(4))

    student_prob = jnp.exp(student_logits - student_lse[:, None])
    gradient = (row_live[:, None] * student_prob * (gap - mean[:, None])).astype(jnp.bfloat16)
    lse_gap = teacher_lse - student_lse
    token_ids = jnp.arange(token_count, dtype=jnp.int32)
    unpack = (token_ids[:, None] == row_token[None, :]).astype(jnp.bfloat16)
    grad_logits = jnp.dot(unpack, gradient, preferred_element_type=jnp.float32).astype(jnp.bfloat16)
    own_ids = dp_index * local_tokens + jnp.arange(local_tokens, dtype=jnp.int32)
    own_of = own_ids[:, None] == row_token[None, :]
    divergence = jnp.sum(jnp.where(own_of, (mean + lse_gap)[None, :], 0.0), axis=1)
    log_ratio = jnp.sum(jnp.where(own_of, (picked + lse_gap)[None, :], 0.0), axis=1)
    return (grad_logits, divergence, log_ratio)


def solution(mesh):
    finer = Mesh(mesh.devices.reshape(8, 4, 8, 2), ("dp_0", "dp_1", "tensor_0", "tensor_1"))
    in_specs = (
        P(DP, TENSOR),
        P(DP, TENSOR),
        P(None, DP_TENSOR),
        P(None, DP_TENSOR),
        P(),
        P(),
        P(),
        P(),
    )
    out_specs = (P(None, DP_TENSOR), P(DP), P(DP))
    return jax.shard_map(
        on_device, mesh=finer, in_specs=in_specs, out_specs=out_specs, check_vma=False
    )
```

```python
import functools
import math

import jax
import jax.numpy as jnp
import numpy as np
from jax import lax
from jax.experimental import pallas as pl
from jax.experimental.pallas import tpu as pltpu
from jax.sharding import Mesh
from jax.sharding import PartitionSpec as P


SLOT = 8
LIVE_DEV = 8
DP = ("dp_0", "dp_1")
TENSOR = ("tensor_0", "tensor_1")
DP_TENSOR = ("dp_0", "dp_1", "tensor_0", "tensor_1")


def spread(array, axes):
    count = lax.axis_size(axes)
    return lax.all_to_all(jnp.broadcast_to(array, (count, *array.shape)), axes, 0, 0)


def shifted(array, axis, by):
    count = lax.axis_size(axis)
    return lax.ppermute(array, axis, [(i, (i + by) % count) for i in range(count)])


def ids_of(axes):
    return np.arange(math.prod(lax.axis_size(a) for a in axes)).reshape([lax.axis_size(a) for a in axes])


def stepped(array, by):
    ids = ids_of(DP_TENSOR)
    after = ids.copy()
    after[..., 0] = np.roll(ids[..., 0], -by, axis=2)
    after[..., 1] = np.roll(ids[..., 1], -by, axis=0)
    perm = list(zip(ids.reshape(-1).tolist(), after.reshape(-1).tolist()))
    return lax.ppermute(array, DP_TENSOR, perm)


def plane_groups():
    ids = ids_of(DP_TENSOR)
    zero = ids[..., 0].transpose(2, 0, 1).reshape(ids.shape[2], -1)
    one = ids[..., 1].transpose(0, 2, 1).reshape(ids.shape[0], -1)
    return np.concatenate([zero, one]).tolist()


def ring_pieces(piece):
    ahead_2, behind_2 = stepped(piece, 2), stepped(piece, -2)
    ahead_1, behind_1 = stepped(piece, 1), stepped(piece, -1)
    ahead_3, across, behind_3 = stepped(ahead_2, 1), stepped(ahead_2, 2), stepped(behind_2, -1)
    return [
        (0, piece),
        (-1, ahead_1),
        (1, behind_1),
        (-2, ahead_2),
        (2, behind_2),
        (-3, ahead_3),
        (3, behind_3),
        (-4, across),
    ]


VMEM = pl.BlockSpec(memory_space=pltpu.VMEM)
SMEM = pl.BlockSpec(memory_space=pltpu.SMEM)


def pick_kernel(lengths, teacher, student, keep, give):
    group = lax.axis_index("dp_0") * lax.axis_size("dp_1") + lax.axis_index("dp_1")
    first, second = lengths[2 * group], lengths[2 * group + 1]
    half, s_width, t_width = student.shape[0] // 2, student.shape[1], teacher.shape[1]
    grid = (LIVE_DEV, teacher.shape[0])
    slot, row = (lax.broadcasted_iota(jnp.int32, grid, d) for d in range(2))
    place = jnp.where(slot < first, slot, SLOT + slot - first)
    pick = jnp.where((place == row) & (slot < first + second), 1.0, 0.0)
    chosen = jnp.dot(
        pick.astype(jnp.bfloat16), teacher[...], preferred_element_type=jnp.float32
    ).astype(jnp.bfloat16)

    def write(students, teachers):
        students[:, :s_width] = student[:half, :]
        students[:, s_width:] = student[half:, :]
        teachers[...] = jnp.zeros(teachers.shape, teachers.dtype)
        teachers[:, :t_width] = chosen

    core = lax.axis_index("tensor_1")
    pl.when(core == 0)(lambda: write(keep, give))
    pl.when(core == 1)(lambda: write(give, keep))


def pack_kernel(s_width, t_width, keep, got, packed):
    core = lax.axis_index("tensor_1")

    @pl.when(core == 0)
    def _():
        for i in range(packed.shape[0]):
            for k, part in enumerate((keep, got)):
                packed[i, :, k * s_width : (k + 1) * s_width] = part[:, :s_width]
                packed[i, :, (2 + k) * s_width : (3 + k) * s_width] = part[:, s_width:]

    @pl.when(core == 1)
    def _():
        for i in range(packed.shape[0]):
            packed[i, :, :t_width] = got[:, :t_width]
            packed[i, :, t_width : 2 * t_width] = keep[:, :t_width]
            packed[i, :, 2 * t_width :] = jnp.zeros(
                (packed.shape[1], packed.shape[2] - 2 * t_width), packed.dtype
            )


def choose_kernel(half, source, gain, everyone, piece, gains):
    count, width = everyone.shape
    s_wide = width // 2
    core = lax.axis_index("tensor_1")
    gains[...] = gain[...]

    @pl.when(core == 0)
    def _():
        j = lax.broadcasted_iota(jnp.int32, (count, count), 1)
        low = (j // half) * (2 * half) + j % half
        want = jnp.broadcast_to(source[:, :1], (count, count))
        one = lambda hit: jnp.where(hit, 1.0, 0.0).astype(jnp.bfloat16)
        dot = functools.partial(jnp.dot, preferred_element_type=jnp.float32)
        chosen = dot(one(want == low), everyone[:, :s_wide])
        chosen += dot(one(want == low + half), everyone[:, s_wide:])
        piece[:, :s_wide] = chosen.astype(jnp.bfloat16)
        piece[:, s_wide:] = jnp.zeros((count, piece.shape[1] - s_wide), piece.dtype)

    @pl.when(core == 1)
    def _():
        piece[...] = everyone[:, : piece.shape[1]]


def block_kernel(offsets, had, s_wide, *refs):
    n = len(offsets)
    blocks, (gains, own, twin), refs = refs[:n], refs[n : n + 3], refs[n + 3 :]
    before, (keep, give, own_buf, twin_buf, sems) = (refs[:2] if had else ()), refs[-5:]
    bufs = (own_buf, twin_buf)

    def fetch(starts, size):
        copies = []
        for i, start in enumerate(starts):
            at = pl.ds(start, size)
            copies.append(
                [
                    pltpu.make_async_copy(head.at[at, :], buf.at[at, :], sems.at[i, k])
                    for k, (head, buf) in enumerate(zip((own, twin), bufs))
                ]
            )
            for copy in copies[-1]:
                copy.start()
        return copies

    rows, t_wide = blocks[0].shape
    dot = functools.partial(jnp.dot, preferred_element_type=jnp.float32)
    core = lax.axis_index("tensor_1")

    @pl.when(core == 0)
    def _():
        y, ys = lax.axis_index("tensor_0"), lax.axis_size("tensor_0")
        totals = [ref[...] for ref in before] if had else [0.0, 0.0]
        starts = [
            pl.multiple_of(lax.rem(y + offset % ys, ys) * s_wide, s_wide) for offset in offsets
        ]
        for block, start, copies in zip(blocks, starts, fetch(starts, s_wide)):
            for copy in copies:
                copy.wait()
            student, features = block[:, :s_wide], pl.ds(start, s_wide)
            totals = [total + dot(student, buf[features, :]) for total, buf in zip(totals, bufs)]
        keep[...], give[...] = totals

    @pl.when(core == 1)
    def _():
        z, zs = lax.axis_index("dp_0"), lax.axis_size("dp_0")
        for k, ref in enumerate((keep, give)):
            ref[...] = before[k][...] if had else jnp.zeros(ref.shape, ref.dtype)
        ys = lax.axis_size("tensor_0")
        copies = fetch([k * t_wide for k in range(ys)], t_wide)
        count = rows // ys
        part = lambda k: jnp.concatenate(
            [block[k * count : (k + 1) * count, :] for block in blocks], axis=0
        ).astype(jnp.float32)
        squares = 0.0
        for k in range(ys):
            values = part(k)
            squares += jnp.sum(values * values, axis=1, keepdims=True)
        row_scale = lax.rsqrt(squares / (ys * t_wide) + 1e-06)
        totals = [0.0, 0.0]
        for k in range(ys):
            normed = (part(k) * row_scale * gains[k : k + 1, :]).astype(jnp.bfloat16)
            for copy in copies[k]:
                copy.wait()
            features = slice(k * t_wide, (k + 1) * t_wide)
            totals = [total + dot(normed, buf[features, :]) for total, buf in zip(totals, bufs)]
        for i, offset in enumerate(offsets):
            at = pl.multiple_of(lax.rem(z + offset % zs, zs) * count, count)
            for ref, total in zip((keep, give), totals):
                ref[pl.ds(at, count), :] = total[i * count : (i + 1) * count, :]


def block_products(found, gains, heads, s_wide, before):
    offsets, blocks = [f[0] for f in found], [f[1] for f in found]
    rows, vocab = blocks[0].shape[0], heads[0].shape[1]
    shape = jax.ShapeDtypeStruct((rows, vocab), jnp.float32)
    return pl.pallas_call(
        functools.partial(block_kernel, offsets, bool(before), s_wide),
        out_shape=(shape, shape),
        in_specs=[VMEM] * (len(blocks) + 1) + [ANY, ANY] + [VMEM] * len(before),
        out_specs=(VMEM, VMEM),
        scratch_shapes=[
            pltpu.VMEM(heads[0].shape, jnp.bfloat16),
            pltpu.VMEM(heads[0].shape, jnp.bfloat16),
            pltpu.SemaphoreType.DMA((lax.axis_size("tensor_0"), 2)),
        ],
        compiler_params=pltpu.CompilerParams(vmem_limit_bytes=LIMIT),
        cost_estimate=pl.CostEstimate(
            flops=4 * len(blocks) * rows * vocab * s_wide,
            bytes_accessed=4 * len(blocks) * vocab * s_wide,
            transcendentals=0,
        ),
    )(*blocks, gains, *heads, *before)


LIMIT = 48 << 20
ANY = pl.BlockSpec(memory_space=pl.ANY)


def merge(parts):
    teacher, student, mean, picked = (parts[:, k] for k in range(4))
    top_t, top_s = jnp.max(teacher, axis=0), jnp.max(student, axis=0)
    sum_t = jnp.sum(jnp.exp(teacher - top_t), axis=0)
    weight = jnp.exp(student - top_s)
    sum_s = jnp.sum(weight, axis=0)
    mean = jnp.sum(weight * mean, axis=0) / sum_s
    return jnp.stack([top_t + jnp.log(sum_t), top_s + jnp.log(sum_s), mean, jnp.sum(picked, axis=0)])


def on_device(
    teacher_hidden,
    student_hidden,
    teacher_head,
    student_head,
    teacher_gain,
    lengths,
    student_row,
    targets,
):
    dp_count = lax.axis_size(DP)
    tensor_count = lax.axis_size(TENSOR)
    y_count, core_count = (lax.axis_size(a) for a in TENSOR)
    local_tokens, t_width = teacher_hidden.shape
    s_width = student_hidden.shape[1]
    token_count = local_tokens * dp_count
    vocab_local = teacher_head.shape[1]
    dp_index = lax.axis_index(DP)
    core = lax.axis_index("tensor_1")
    vocab_start = (dp_index * tensor_count + lax.axis_index(TENSOR)) * vocab_local

    first, second = lengths.reshape(dp_count, 2)[:, :1], lengths.reshape(dp_count, 2)[:, 1:]
    slot = jnp.arange(LIVE_DEV, dtype=jnp.int32)[None, :]
    place = jnp.where(slot < first, slot, SLOT + slot - first)
    live = slot < first + second
    group = jnp.arange(dp_count, dtype=jnp.int32)[:, None] * local_tokens
    row_token = jnp.where(live, group + place, -1).reshape(-1)
    row_live = live.reshape(-1).astype(jnp.float32)
    rows = row_token.shape[0]

    half = local_tokens // 2
    s_wide, t_wide = s_width * core_count, t_width * core_count
    pair = jax.ShapeDtypeStruct((half, 2 * s_width), jnp.bfloat16)
    small = pltpu.CompilerParams(vmem_limit_bytes=8 << 20)
    keep, give = pl.pallas_call(
        pick_kernel,
        out_shape=(pair, pair),
        in_specs=[SMEM, VMEM, VMEM],
        out_specs=(VMEM, VMEM),
        compiler_params=pltpu.CompilerParams(vmem_limit_bytes=62 << 20),
    )(lengths, teacher_hidden, student_hidden)
    packed = pl.pallas_call(
        functools.partial(pack_kernel, s_width, t_width),
        out_shape=jax.ShapeDtypeStruct((dp_count, half, 2 * s_wide), jnp.bfloat16),
        in_specs=[VMEM, VMEM],
        out_specs=VMEM,
        compiler_params=pltpu.CompilerParams(vmem_limit_bytes=62 << 20),
    )(keep, shifted(give, "tensor_1", 1))
    everyone = lax.all_to_all(packed, DP_TENSOR, 0, 0, axis_index_groups=plane_groups())
    tall = jnp.pad(student_head, ((0, t_wide * y_count - s_wide * y_count), (0, 0)))
    away = jnp.where(core == 0, teacher_head, tall)
    own = jnp.where(core == 0, tall, teacher_head)
    heads = (own, shifted(away, "tensor_1", 1))
    gains = teacher_gain.reshape(y_count, t_wide)

    token_of = row_token[:, None] == jnp.arange(token_count, dtype=jnp.int32)[None, :]
    row_source = jnp.sum(jnp.where(token_of, student_row[None, :], 0), axis=1)
    row_target = jnp.sum(jnp.where(token_of, targets[None, :], 0), axis=1)
    piece, gains = pl.pallas_call(
        functools.partial(choose_kernel, half),
        out_shape=(
            jax.ShapeDtypeStruct((rows, t_wide), jnp.bfloat16),
            jax.ShapeDtypeStruct(gains.shape, jnp.float32),
        ),
        in_specs=[VMEM] * 3,
        out_specs=(VMEM, VMEM),
        compiler_params=small,
    )(jnp.broadcast_to(row_source[:, None], (rows, 128)), gains, everyone.reshape(rows, -1))

    found = ring_pieces(piece)
    parts = block_products(found[:5], gains, heads, s_wide, ())
    kept, sent = block_products(found[5:], gains, heads, s_wide, parts)
    got = shifted(sent, "tensor_1", 1)
    student_logits = jnp.where(core == 0, kept, got)
    teacher_logits = jnp.where(core == 0, got, kept)

    gap = student_logits - teacher_logits
    hits = (row_target - vocab_start)[:, None] == jnp.arange(vocab_local, dtype=jnp.int32)[None, :]
    picked = jnp.sum(jnp.where(hits, gap, 0.0), axis=1)
    teacher_max = jnp.max(teacher_logits, axis=1)
    student_max = jnp.max(student_logits, axis=1)
    teacher_sum = jnp.sum(jnp.exp(teacher_logits - teacher_max[:, None]), axis=1)
    student_exp = jnp.exp(student_logits - student_max[:, None])
    student_sum = jnp.sum(student_exp, axis=1)
    mean = jnp.sum(student_exp * gap, axis=1) / student_sum
    local = jnp.stack(
        [teacher_max + jnp.log(teacher_sum), student_max + jnp.log(student_sum), mean, picked]
    )
    merged, dp_late = lax.optimization_barrier(
        (spread(merge(spread(local, DP)), TENSOR), dp_index)
    )
    merged = merge(merged)
    teacher_lse, student_lse, mean, picked = (merged[k] for k in range(4))

    student_prob = jnp.exp(student_logits - student_lse[:, None])
    gradient = (row_live[:, None] * student_prob * (gap - mean[:, None])).astype(jnp.bfloat16)
    lse_gap = teacher_lse - student_lse
    token_ids = jnp.arange(token_count, dtype=jnp.int32)
    unpack = (token_ids[:, None] == row_token[None, :]).astype(jnp.bfloat16)
    grad_logits = jnp.dot(unpack, gradient, preferred_element_type=jnp.float32).astype(jnp.bfloat16)
    own_ids = dp_late * local_tokens + jnp.arange(local_tokens, dtype=jnp.int32)
    own_of = own_ids[:, None] == row_token[None, :]
    divergence = jnp.sum(jnp.where(own_of, (mean + lse_gap)[None, :], 0.0), axis=1)
    log_ratio = jnp.sum(jnp.where(own_of, (picked + lse_gap)[None, :], 0.0), axis=1)
    return (grad_logits, divergence, log_ratio)


def solution(mesh):
    finer = Mesh(mesh.devices.reshape(8, 4, 8, 2), ("dp_0", "dp_1", "tensor_0", "tensor_1"))
    in_specs = (
        P(DP, TENSOR),
        P(DP, TENSOR),
        P(None, DP_TENSOR),
        P(None, DP_TENSOR),
        P(),
        P(),
        P(),
        P(),
    )
    out_specs = (P(None, DP_TENSOR), P(DP), P(DP))
    return jax.shard_map(
        on_device, mesh=finer, in_specs=in_specs, out_specs=out_specs, check_vma=False
    )
```
